32 devices in a mesh: group: 2 (over y), branch: 4 (over x, core), tensor: 4 (over z).
Axes of the slice: x: 2, y: 2, z: 4, core: 2. Of those that a mesh axis runs over, the one named last changes fastest.
Arguments:
- queries: bfloat16 [2048, 8192], P(('group', 'branch'), 'tensor'), parts along dimension 0, may hold values from -160 to 160
- prefix_cache: bfloat16 [2, 3072, 1024], P(None, 'group', 'tensor'), parts along dimension 1, may hold values from -5 to 5
- prior_cache: bfloat16 [2, 2048, 1024], P(None, ('group', 'branch'), 'tensor'), parts along dimension 1, may hold values from -5 to 5
- fresh_cache: bfloat16 [2, 2048, 1024], P(None, ('group', 'branch'), 'tensor'), parts along dimension 1, may hold values from -5 to 5
- visible: int32 [8, 4], P('group'), parts along dimension 0, may hold values 0 or 1
- turn_order: int32 [8], P('group'), parts along dimension 0, may hold values from 0 to 3, each once
- output_weight: bfloat16 [8192, 8192], P('tensor', 'branch'), may hold values from -0.0625 to 0.0625
Outputs:
- projected: bfloat16 [2048, 8192], P(('group', 'branch'), 'tensor'), parts along dimension 0
The draws below stay inside these ranges and needn't reach their ends.
There are 2 independent parts, one for each index of `group`. The reference program is written for one: setup_inputs(seed, part) draws one part's arguments, and reference() takes and returns one part's arrays. A program takes and returns all parts, laid end to end along the dimension named above; an argument that names none is the same for every part. Nothing has to cross between parts.
Inputs may be any that keep to these rules, and one draw needn't show every extreme that they name: `turn_order`: each of 0 to 3 once.
All inputs are finite; a program needn't handle non-finite values.
Results may differ from the reference program's by a relative error of at most 0.015.
Values may be sent and summed in bfloat16 or wider, within the bound.
No kernel may reach another device: no remote copies, remote signals or barrier semaphores. Data moves between devices by JAX's collectives and lax.ppermute only.
A program may use at most 64 MiB of HBM per device.

```python
import math
import jax
import jax.numpy as jnp
from jax import lax

D = 8192
H = 64
KVH = 8
HD = 128
MSG = 256
PREFIX = 1536
AGENTS = 4
TOKENS = 1024
QW = 8192
KVW = 1024
N_BRANCH = 4
N_TENSOR = 4


def shared_prefix(key):
    base_key = jax.random.fold_in(key, 7)
    cache = jnp.clip(jax.random.normal(jax.random.fold_in(base_key, 1), (2, PREFIX, KVH * HD), jnp.float32), -5.0, 5.0)
    return cache


def draw_prefix_cache(key, part):
    cache = shared_prefix(key)
    return cache.astype(jnp.bfloat16)


def draw_queries(key, part):
    values = jnp.clip(jax.random.normal(jax.random.fold_in(key, 4), (TOKENS, H * HD), jnp.float32) * 2.5, -15.0, 15.0)
    return values.astype(jnp.bfloat16)


def place_ends(result, own_key, low, high):
    longest = result.shape.index(max(result.shape))
    spots = []
    for shift in (0, 1):
        where = [jax.random.randint(jax.random.fold_in(own_key, axis), (), 0, length) for axis, length in enumerate(result.shape)]
        where[longest] = (where[longest] + shift) % result.shape[longest]
        spots.append(tuple(where))
    return result.at[spots[0]].set(low).at[spots[1]].set(high)


def steps_of(key, extent, cuts, smallest, high):
    factor_of, own = 1.0, jax.random.fold_in(key, 6)
    for axis_at, parts in cuts:
        draws = jnp.exp(jax.random.uniform(jax.random.fold_in(own, axis_at), (parts,), jnp.float32, smallest / len(cuts), high / len(cuts)))
        factor_of = factor_of * jnp.repeat(draws, extent[axis_at] // parts).reshape([-1 if axis == axis_at else 1 for axis in range(len(extent))])
    return factor_of


def normal_values(stream_key, shape, spread, most, cuts=(), kind=jnp.bfloat16):
    result = jax.random.normal(stream_key, shape, jnp.float32) * spread
    if len(cuts) > 0:
        result = steps_of(stream_key, shape, cuts, -0.22, 0.18) * result
    return jnp.clip(result, min=-most, max=most).astype(kind)


def setup_inputs(seed: int = 0, part: int = 0) -> dict:
    splits = jax.random.split(jax.random.key(seed), 8)
    own_keys = jax.random.split(jax.random.fold_in(splits[7], part), 8)
    queries = draw_queries(jax.random.fold_in(jax.random.fold_in(splits[7], part), 71), part)
    prefix_cache = draw_prefix_cache(jax.random.fold_in(jax.random.fold_in(splits[7], part), 71), part)
    prior_cache = normal_values(own_keys[2], (2, TOKENS, KVW), 1.0, 5.0, ((1, 4), (2, 4)))
    fresh_cache = normal_values(own_keys[3], (2, TOKENS, KVW), 1.0, 5.0, ((1, 4), (2, 4)))
    visible = place_ends((jax.random.randint(own_keys[4], (AGENTS, AGENTS), 0, 2) < 1).astype(jnp.int32), jax.random.fold_in(own_keys[4], 1), 0, 1)
    turn_order = jax.random.permutation(own_keys[5], AGENTS).astype(jnp.int32)
    output_weight = normal_values(splits[6], (QW, D), QW ** -0.5, 0.0625, ((0, 4), (1, 4)))
    return dict(queries=queries, prefix_cache=prefix_cache, prior_cache=prior_cache, fresh_cache=fresh_cache, visible=visible, turn_order=turn_order, output_weight=output_weight)


NEGATIVE = -1e+30

def reference(queries, prefix_cache, prior_cache, fresh_cache, visible, turn_order, output_weight):
    sharing = H // KVH
    key_rows = jnp.concatenate([prefix_cache[0], prior_cache[0], fresh_cache[0]], axis=0).reshape(-1, KVH, HD)
    value_rows = jnp.concatenate([prefix_cache[1], prior_cache[1], fresh_cache[1]], axis=0).reshape(-1, KVH, HD)
    message_index = jnp.arange(TOKENS, dtype=jnp.int32)
    owner_ids = message_index // MSG
    offsets = message_index % MSG
    positions = jnp.arange(MSG, dtype=jnp.int32)

    def one_agent(agent_id):
        query_rows = lax.dynamic_slice_in_dim(queries, agent_id * MSG, MSG, 0).reshape(MSG, KVH, sharing, HD)
        prior_seen = visible[agent_id][owner_ids] == 1
        fresh_seen = (turn_order[owner_ids] < turn_order[agent_id])[None, :] | (owner_ids == agent_id)[None, :] & (offsets[None, :] <= positions[:, None])
        allowed = jnp.concatenate([jnp.ones((MSG, PREFIX), jnp.bool_), jnp.broadcast_to(prior_seen[None, :], (MSG, TOKENS)), fresh_seen], axis=1)

        def one_group(group_id):
            query_group = lax.dynamic_index_in_dim(query_rows, group_id, 1, False).astype(jnp.float32)
            key_group = lax.dynamic_index_in_dim(key_rows, group_id, 1, False).astype(jnp.float32)
            value_group = lax.dynamic_index_in_dim(value_rows, group_id, 1, False).astype(jnp.float32)
            scores = jnp.einsum('qsd,kd->sqk', query_group, key_group) / math.sqrt(HD)
            masked = jnp.where(allowed[None], scores, NEGATIVE)
            row_peak = lax.optimization_barrier(jnp.max(masked, axis=-1, keepdims=True))
            weights = jnp.where(allowed[None], jnp.exp(masked - row_peak), 0.0)
            row_total = lax.optimization_barrier(jnp.sum(weights, axis=-1, keepdims=True))
            rounded = lax.optimization_barrier(weights.astype(jnp.bfloat16)).astype(jnp.float32)
            return (jnp.einsum('sqk,kd->sqd', rounded, value_group) / row_total).astype(jnp.bfloat16)
        grouped = lax.map(one_group, jnp.arange(KVH, dtype=jnp.int32))
        return jnp.transpose(grouped, (2, 0, 1, 3)).reshape(MSG, H * HD)
    attention = lax.map(one_agent, jnp.arange(AGENTS, dtype=jnp.int32)).reshape(TOKENS, H * HD)
    block_width = H * HD // N_TENSOR

    def add_block(summed, block_index):
        section = lax.dynamic_slice_in_dim(attention, block_index * block_width, block_width, 1)
        weight_rows = lax.dynamic_slice_in_dim(output_weight, block_index * block_width, block_width, 0)
        product = jnp.dot(section, weight_rows, preferred_element_type=jnp.float32)
        return (summed + lax.optimization_barrier(product.astype(jnp.bfloat16)).astype(jnp.float32), None)
    summed, unused = lax.scan(add_block, jnp.zeros((TOKENS, D), jnp.float32), jnp.arange(N_TENSOR, dtype=jnp.int32))
    rounded_sum = summed.astype(jnp.bfloat16)
    piece_width = D // (N_BRANCH * N_TENSOR)
    return jnp.transpose(rounded_sum.reshape(TOKENS, N_BRANCH, N_TENSOR, piece_width), (0, 2, 1, 3)).reshape(TOKENS, D)
```

```python
import functools
import math

import jax
import jax.numpy as jnp
from jax import lax
from jax.experimental import pallas as pl
from jax.experimental.pallas import tpu as pltpu
from jax.sharding import PartitionSpec as P

HD = 128
NEGATIVE = -1e30
LOG2E = 1.4426950408889634

CHUNK_PARTS = (1, 1, 1, 1)


def exchange(value, axis, size, bit):
    return lax.ppermute(value, axis, [(i, i ^ bit) for i in range(size)])


def cost(flops, reads, exps=0):
    return pl.CostEstimate(
        flops=int(flops), bytes_accessed=int(reads), transcendentals=int(exps)
    )


def scores_of(rows, keys):
    return lax.dot_general(
        rows, keys, (((1,), (1,)), ((), ())), preferred_element_type=jnp.float32
    )


def widen(values):
    return jnp.concatenate([values, jnp.ones_like(values)], axis=1)


def prefix_body(query_ref, cache_ref, state_ref, *, sharing, factor):
    keys = cache_ref[0]
    values = widen(cache_ref[1])
    for head in range(sharing):
        rows = query_ref[:, head * HD : (head + 1) * HD]
        scores = scores_of(rows, keys)
        peak = jnp.max(scores, axis=-1, keepdims=True)
        weights = jnp.exp2((scores - peak) * factor).astype(jnp.bfloat16)
        both = jnp.dot(weights, values, preferred_element_type=jnp.float32)
        lane = lax.broadcasted_iota(jnp.int32, (rows.shape[0], HD), 1)
        state_ref[0, head, :, :HD] = both[:, :HD]
        state_ref[0, head, :, HD:] = jnp.where(lane < HD // 2, peak, both[:, HD:])


def prefix_attention(queries, prefix_cache, groups, sharing):
    rows = queries.shape[0]
    prefix = prefix_cache.shape[1]
    return pl.pallas_call(
        functools.partial(
            prefix_body, sharing=sharing, factor=LOG2E / math.sqrt(HD)
        ),
        grid=(groups,),
        in_specs=[
            pl.BlockSpec((rows, sharing * HD), lambda g: (0, g)),
            pl.BlockSpec((2, prefix, HD), lambda g: (0, 0, g)),
        ],
        out_specs=pl.BlockSpec((1, sharing, rows, 2 * HD), lambda g: (g, 0, 0, 0)),
        out_shape=jax.ShapeDtypeStruct((groups, sharing, rows, 2 * HD), jnp.float32),
        name="prefix",
        cost_estimate=cost(
            8 * groups * sharing * rows * prefix * HD,
            queries.size * 2 + prefix_cache.size * 2 + groups * sharing * rows * 8 * HD,
            groups * sharing * rows * prefix,
        ),
    )(queries, prefix_cache)


def message_body(
    place_ref, visible_ref, turn_ref, query_ref, state_ref, *refs, sharing, counts, offset, factor
):
    pieces = 2 * len(counts)
    caches = refs[:pieces]
    out_ref, stacked, gathered, peaks = refs[pieces:]
    rows = query_ref.shape[0]
    for head in range(sharing):
        at = slice(head * rows, (head + 1) * rows)
        stacked[at, :] = query_ref[:, head * HD : (head + 1) * HD]
        kept = state_ref[0, head]
        gathered[at, :HD] = kept[:, :HD]
        gathered[at, HD:] = jnp.broadcast_to(kept[:, 2 * HD - 1 :], (rows, HD))
        peaks[at, :] = jnp.broadcast_to(kept[:, HD : HD + 1], (rows, HD))
    me = place_ref[0]
    own_turn = turn_ref[me]

    def add_block(keys, values, causal):
        scores = scores_of(stacked[...], keys)
        if causal:
            spot = lax.broadcasted_iota(jnp.int32, scores.shape, 0) % rows + offset
            scores = jnp.where(
                lax.broadcasted_iota(jnp.int32, scores.shape, 1) <= spot, scores, NEGATIVE
            )
        before = peaks[...]
        now = jnp.maximum(before, jnp.max(scores, axis=-1, keepdims=True))
        peaks[...] = now
        wide = jnp.concatenate([now] * (keys.shape[0] // HD), axis=1)
        weights = jnp.exp2((scores - wide) * factor).astype(jnp.bfloat16)
        shrink = jnp.exp2((before - now) * factor)
        gathered[...] = gathered[...] * jnp.concatenate([shrink, shrink], axis=1) + jnp.dot(
            weights, widen(values), preferred_element_type=jnp.float32
        )

    for number, count in enumerate(counts):
        prior_ref, fresh_ref = caches[2 * number : 2 * number + 2]

        def one(index, prior_ref=prior_ref, fresh_ref=fresh_ref, number=number):
            agent = place_ref[2 + number] + index

            @pl.when(visible_ref[me, agent] == 1)
            def _():
                add_block(prior_ref[index, 0], prior_ref[index, 1], False)

            @pl.when(turn_ref[agent] < own_turn)
            def _():
                add_block(fresh_ref[index, 0], fresh_ref[index, 1], False)

            @pl.when(agent == me)
            def _():
                add_block(fresh_ref[index, 0], fresh_ref[index, 1], True)

        if count == 1:
            one(0)
        else:
            lax.fori_loop(0, count, lambda index, carry: (one(index), carry)[1], 0)

    for head in range(sharing):
        at = slice(head * rows, (head + 1) * rows)
        out_ref[:, head * HD : (head + 1) * HD] = (
            gathered[at, :HD] / gathered[at, HD:]
        ).astype(jnp.bfloat16)


def message_attention(place, visible, turn_order, queries, state, caches, rows, offset):
    groups, sharing = state.shape[0], state.shape[1]
    message = caches[0].shape[2]
    counts = tuple(cache.shape[0] for cache in caches[::2])
    agents = sum(counts)
    chunk = offset // rows
    return pl.pallas_call(
        functools.partial(
            message_body,
            sharing=sharing,
            counts=counts,
            offset=offset,
            factor=LOG2E / math.sqrt(HD),
        ),
        grid_spec=pltpu.PrefetchScalarGridSpec(
            num_scalar_prefetch=3,
            grid=(groups,),
            in_specs=[
                pl.BlockSpec((rows, sharing * HD), lambda g, *_: (chunk, g)),
                pl.BlockSpec((1, sharing, rows, 2 * HD), lambda g, *_: (g, 0, chunk, 0)),
            ]
            + [
                pl.BlockSpec((cache.shape[0], 2, message, HD), lambda g, *_: (0, 0, 0, g))
                for cache in caches
            ],
            out_specs=pl.BlockSpec((rows, sharing * HD), lambda g, *_: (0, g)),
            scratch_shapes=[
                pltpu.VMEM((sharing * rows, HD), jnp.bfloat16),
                pltpu.VMEM((sharing * rows, 2 * HD), jnp.float32),
                pltpu.VMEM((sharing * rows, HD), jnp.float32),
            ],
        ),
        out_shape=jax.ShapeDtypeStruct((rows, groups * sharing * HD), jnp.bfloat16),
        name="messages",
        cost_estimate=cost(
            8 * groups * sharing * rows * 2 * agents * message * HD,
            rows * groups * sharing * HD * 12 + agents * message * groups * HD * 8,
            groups * sharing * rows * 2 * agents * message,
        ),
    )(place, visible, turn_order, queries, state, *caches)


def project_body(columns_ref, *refs):
    *row_refs, weight_ref, out_ref = refs
    rows = jnp.concatenate([row_ref[...] for row_ref in row_refs], axis=0)
    out_ref[0] = jnp.dot(
        rows, weight_ref[...], preferred_element_type=jnp.float32
    ).astype(jnp.bfloat16)


def project(columns, pieces, output_weight, width):
    rows, depth = pieces[0].shape
    blocks = columns.shape[0]
    total = rows * len(pieces)
    return pl.pallas_call(
        project_body,
        grid_spec=pltpu.PrefetchScalarGridSpec(
            num_scalar_prefetch=1,
            grid=(blocks,),
            in_specs=[pl.BlockSpec((rows, depth), lambda j, c: (0, 0)) for piece in pieces]
            + [pl.BlockSpec((depth, width), lambda j, c: (0, c[j]))],
            out_specs=pl.BlockSpec((1, total, width), lambda j, c: (j, 0, 0)),
        ),
        out_shape=jax.ShapeDtypeStruct((blocks, total, width), jnp.bfloat16),
        name="project",
        cost_estimate=cost(
            2 * total * depth * width * blocks,
            2 * (total * depth + depth * width * blocks + total * width * blocks),
        ),
    )(columns, *pieces, output_weight)


def place_body(place_ref, *refs):
    pieces = refs[:-1] if len(refs) % 2 else refs[:-2]
    out_ref = refs[-1]
    width = pieces[0].shape[1]
    for number, piece in enumerate(pieces):
        at = pl.multiple_of((place_ref[0] ^ number) * width, width)
        out_ref[:, pl.ds(at, width)] = piece[...]


def place_columns(place, pieces, whole, message, offset):
    rows, width = pieces[0].shape
    columns = width * len(pieces)
    chunk = offset // rows
    specs = [pl.BlockSpec((rows, width), lambda i, p: (0, 0)) for piece in pieces]
    operands = list(pieces)
    aliases = {}
    if whole is not None:
        specs.append(pl.BlockSpec(memory_space=pl.ANY))
        operands.append(whole)
        aliases = {len(operands): 0}
    return pl.pallas_call(
        place_body,
        grid_spec=pltpu.PrefetchScalarGridSpec(
            num_scalar_prefetch=1,
            grid=(1,),
            in_specs=specs,
            out_specs=pl.BlockSpec((rows, columns), lambda i, p: (chunk, 0)),
        ),
        out_shape=jax.ShapeDtypeStruct((message, columns), jnp.bfloat16),
        input_output_aliases=aliases,
        name="place",
        cost_estimate=cost(0, 4 * rows * columns),
    )(place, *operands)


def spread(value, axis, size):
    pieces = {0: value}
    bit = size // 2
    while bit:
        for offset in list(pieces):
            pieces[offset | bit] = exchange(pieces[offset], axis, size, bit)
        bit //= 2
    return [pieces[offset] for offset in range(size)]


def wide(value):
    return value.astype(jnp.float32)


def finish(attention, output_weight):
    product = jnp.dot(
        lax.all_gather(attention, "branch", axis=0, tiled=True),
        output_weight,
        preferred_element_type=jnp.float32,
    )
    column_totals = lax.psum_scatter(
        product.astype(jnp.bfloat16), "tensor", scatter_dimension=1, tiled=True
    )
    return lax.all_to_all(column_totals, "branch", split_axis=0, concat_axis=1, tiled=True)


def per_device(
    branches,
    tensors,
    queries,
    prefix_cache,
    prior_cache,
    fresh_cache,
    visible,
    turn_order,
    output_weight,
):
    message = queries.shape[0]
    groups = prefix_cache.shape[2] // HD
    sharing = queries.shape[1] // HD // groups
    width = output_weight.shape[1] // tensors
    agent = lax.axis_index("branch").astype(jnp.int32)
    slot = lax.axis_index("tensor").astype(jnp.int32)
    powers = all(size & (size - 1) == 0 for size in (branches, tensors))
    chunked = powers and branches <= 4 and tensors > 1 and width % HD == 0

    if not chunked:
        caches = (
            jnp.swapaxes(lax.all_gather(prior_cache, "branch", axis=1, tiled=False), 0, 1),
            jnp.swapaxes(lax.all_gather(fresh_cache, "branch", axis=1, tiled=False), 0, 1),
        )
        place = jnp.stack([agent, slot, jnp.int32(0)])
        state = prefix_attention(queries, prefix_cache, groups, sharing)
        rows = message // 4
        attention = jnp.concatenate(
            [
                message_attention(
                    place, visible, turn_order, queries, state, caches, rows, offset
                )
                for offset in range(0, message, rows)
            ],
            axis=0,
        )
        return finish(attention, output_weight)

    others = jnp.arange(branches, dtype=jnp.int32) ^ agent
    place = jnp.concatenate([agent[None], slot[None], others])
    steps = jnp.arange(tensors, dtype=jnp.int32)
    sent_columns = slot ^ (2 * steps[: tensors // 2] + 1)
    kept_columns = slot ^ (2 * steps[: tensors // 2])

    prior = spread(prior_cache, "branch", branches)
    fresh = spread(fresh_cache, "branch", branches)
    state = prefix_attention(queries, prefix_cache, groups, sharing)
    caches = [cache[None] for pair in zip(prior, fresh) for cache in pair]

    unit = message // sum(CHUNK_PARTS)
    result = None
    offset = 0
    for part in CHUNK_PARTS:
        rows = unit * part
        attention = message_attention(
            place, visible, turn_order, queries, state, caches, rows, offset
        )
        pieces = spread(attention, "branch", branches)
        sent = project(sent_columns, pieces, output_weight, width)
        arrived = exchange(sent, "tensor", tensors, 1)
        kept = project(kept_columns, pieces, output_weight, width)
        total = wide(kept) + wide(arrived)
        bit = 2
        while bit < tensors:
            arrived = exchange(total[1::2].astype(jnp.bfloat16), "tensor", tensors, bit)
            total = total[0::2] + wide(arrived)
            bit *= 2
        summed = total[0].astype(jnp.bfloat16).reshape(branches, rows, width)
        columns = [
            exchange(summed[number], "branch", branches, number) if number else summed[0]
            for number in range(branches)
        ]
        result = place_columns(place, columns, result, message, offset)
        offset += rows
    return result


def solution(mesh):
    return jax.shard_map(
        functools.partial(per_device, mesh.shape["branch"], mesh.shape["tensor"]),
        mesh=mesh,
        in_specs=(
            P(("group", "branch"), "tensor"),
            P(None, "group", "tensor"),
            P(None, ("group", "branch"), "tensor"),
            P(None, ("group", "branch"), "tensor"),
            P("group", None),
            P("group"),
            P("tensor", "branch"),
        ),
        out_specs=P(("group", "branch"), "tensor"),
        check_vma=False,
    )
```
